32 devices in a mesh: groups: 2 (over x), tile: 16 (over z, y, core).
Axes of the slice: x: 2, y: 2, z: 4, core: 2. Of those that a mesh axis runs over, the one named last changes fastest.
Arguments:
- features: bfloat16 [8, 384, 16, 8, 16], P('groups', None, 'tile'), parts along dimension 0, may hold values from -6 to 6
- cache_first: bfloat16 [4, 384, 16, 8, 16], P('groups', None, 'tile'), parts along dimension 0, may hold values from -6 to 6
- cache_second: bfloat16 [4, 192, 16, 16, 32], P('groups', None, 'tile'), parts along dimension 0, may hold values from -6 to 6
- cache_third: bfloat16 [4, 96, 16, 32, 64], P('groups', None, 'tile'), parts along dimension 0, may hold values from -6 to 6
- weight_first: bfloat16 [3, 3, 3, 192, 384], replicated, may hold values from -0.0625 to 0.0625
- weight_second: bfloat16 [3, 3, 3, 96, 192], replicated, may hold values from -0.078125 to 0.078125
- weight_third: bfloat16 [3, 3, 3, 3, 96], replicated, may hold values from -0.125 to 0.125
- gain_first: float32 [384], replicated, may hold values from 0.1 to 1.9
- gain_second: float32 [192], replicated, may hold values from 0.1 to 1.9
- gain_third: float32 [96], replicated, may hold values from 0.1 to 1.9
Outputs:
- pixels: float32 [8, 3, 16, 32, 64], P('groups', None, 'tile'), parts along dimension 0
The draws below stay inside these ranges and needn't reach their ends.
There are 2 independent parts, one for each index of `groups`. The reference program is written for one: setup_inputs(seed, part) draws one part's arguments, and reference() takes and returns one part's arrays. A program takes and returns all parts, laid end to end along the dimension named above; an argument that names none is the same for every part. Nothing has to cross between parts.
All inputs are finite; a program needn't handle non-finite values.
Results may differ from the reference program's by a relative error of at most 0.0085.
Values may be sent and summed in bfloat16 or wider, within the bound.
A program may use at most 64 MiB of HBM per device.

```python
import jax
import jax.numpy as jnp
from jax import lax

C1 = 384
C2 = 192
C3 = 96
RGB = 3
TILES_X = 8
TILE_H = 8
TILE_W = 16
FRAMES = 4
N_TILE = 16


def shard_levels(stream_key, shape, cuts, least, top_value):
    factor_of = 1.0
    for dim, blocks in cuts:
        steps = jax.random.uniform(jax.random.fold_in(jax.random.fold_in(stream_key, 6), dim), (blocks,), jnp.float32, least / len(cuts), top_value / len(cuts))
        factor_of = factor_of * jnp.repeat(jnp.exp(steps), shape[dim] // blocks).reshape((-1,) + (1,) * (len(shape) - 1 - dim))
    return factor_of


def scatter_about(stream_key, dims, scale, limit, shards=(), kind=jnp.bfloat16):
    level = shard_levels(stream_key, dims, shards, -0.22, 0.18) if shards else 1.0
    values = jax.random.normal(stream_key, dims, jnp.float32) * scale * level
    return jnp.minimum(jnp.maximum(values, -limit), limit).astype(kind)


def setup_inputs(seed: int = 0, part: int = 0) -> dict:
    streams_of = jax.random.split(jax.random.key(seed), 11)
    part_splits = jax.random.split(jax.random.fold_in(streams_of[10], part), 11)
    features = scatter_about(part_splits[0], (FRAMES, C1, N_TILE, TILE_H, TILE_W), 1.0, 6.0, ((2, 16),))
    cache_first = scatter_about(part_splits[1], (2, C1, N_TILE, TILE_H, TILE_W), 1.0, 6.0, ((2, 16),))
    cache_second = scatter_about(part_splits[2], (2, C2, N_TILE, 2 * TILE_H, 2 * TILE_W), 1.0, 6.0, ((2, 16),))
    cache_third = scatter_about(part_splits[3], (2, C3, N_TILE, 4 * TILE_H, 4 * TILE_W), 1.0, 6.0, ((2, 16),))
    weight_first = scatter_about(streams_of[4], (3, 3, 3, C2, C1), (27 * C1) ** -0.5, 0.0625)
    weight_second = scatter_about(streams_of[5], (3, 3, 3, C3, C2), (27 * C2) ** -0.5, 0.078125)
    weight_third = scatter_about(streams_of[6], (3, 3, 3, RGB, C3), (27 * C3) ** -0.5, 0.125)
    gain_first = jnp.clip(1.0 + 0.18 * jax.random.normal(streams_of[7], (C1,), jnp.float32), 0.1, 1.9)
    gain_second = jnp.clip(1.0 + 0.18 * jax.random.normal(streams_of[8], (C2,), jnp.float32), 0.1, 1.9)
    gain_third = jnp.clip(1.0 + 0.18 * jax.random.normal(streams_of[9], (C3,), jnp.float32), 0.1, 1.9)
    return {"features": features, "cache_first": cache_first, "cache_second": cache_second, "cache_third": cache_third, "weight_first": weight_first, "weight_second": weight_second, "weight_third": weight_third, "gain_first": gain_first, "gain_second": gain_second, "gain_third": gain_third}


epsilon = 1e-06

def assemble(values):
    values = jnp.roll(values, TILES_X // 2, axis=2)
    frames, chans, count, height, width = values.shape
    tall = count // TILES_X
    grid = values.reshape(frames, chans, tall, TILES_X, height, width)
    return grid.transpose(0, 1, 2, 4, 3, 5).reshape(frames, chans, tall * height, TILES_X * width)

def split_tiles(values, height, width):
    frames, chans, total_rows, total_cols = values.shape
    grid = values.reshape(frames, chans, total_rows // height, height, TILES_X, width)
    tiled = grid.transpose(0, 1, 2, 4, 3, 5).reshape(frames, chans, total_rows // height * TILES_X, height, width)
    return jnp.roll(tiled, -(TILES_X // 2), axis=2)

def activate(values, gain):
    widened = values.astype(jnp.float32)
    meansq = lax.optimization_barrier(jnp.mean(widened * widened, axis=1, keepdims=True))
    normed = widened * lax.rsqrt(meansq + epsilon) * gain.astype(jnp.float32)[None, :, None, None]
    return jax.nn.silu(normed).astype(jnp.bfloat16)

def enlarge(values):
    return jnp.repeat(jnp.repeat(values, 2, axis=2), 2, axis=3)

def convolve(stacked, weight):
    frame_count = stacked.shape[0] - 2
    row_count = stacked.shape[2]
    col_count = stacked.shape[3]
    padded = jnp.pad(stacked, ((0, 0), (0, 0), (1, 1), (1, 1)))
    widened_weight = weight.astype(jnp.float32)

    def single(frame_index):
        slab = lax.dynamic_slice_in_dim(padded, frame_index, 3, 0).astype(jnp.float32)
        total = jnp.zeros((weight.shape[3], row_count, col_count), jnp.float32)
        for tap_time in range(3):
            for tap_row in range(3):
                for tap_col in range(3):
                    window = slab[tap_time, :, tap_row:tap_row + row_count, tap_col:tap_col + col_count]
                    total = total + jnp.einsum('oc,chw->ohw', widened_weight[tap_time, tap_row, tap_col], window)
        return total
    return lax.map(single, jnp.arange(frame_count, dtype=jnp.int32))

def reference(features, cache_first, cache_second, cache_third, weight_first, weight_second, weight_third, gain_first, gain_second, gain_third):
    inputs_first = activate(assemble(features), gain_first)
    out_first = convolve(jnp.concatenate([assemble(cache_first), inputs_first], 0), weight_first).astype(jnp.bfloat16)
    inputs_second = activate(enlarge(out_first), gain_second)
    out_second = convolve(jnp.concatenate([assemble(cache_second), inputs_second], 0), weight_second).astype(jnp.bfloat16)
    inputs_third = activate(enlarge(out_second), gain_third)
    result = convolve(jnp.concatenate([assemble(cache_third), inputs_third], 0), weight_third)
    return split_tiles(result, 4 * TILE_H, 4 * TILE_W)
```

```python
import functools

import jax
import jax.numpy as jnp
import numpy as np
from jax import lax
from jax.experimental import pallas as pl
from jax.experimental.pallas import tpu as pltpu
from jax.sharding import PartitionSpec as P

TILES_X = 8
epsilon = 1e-06
MESH = pl.DeviceIdType.MESH
DIRS = ((1, 0), (-1, 0), (1, 1), (1, -1), (-1, 1), (-1, -1), (0, 1), (0, -1))
BF = jnp.bfloat16
F32 = jnp.float32
NT = (((1,), (1,)), ((), ()))


def position(count):
    placed = lax.rem(lax.axis_index("tile") + TILES_X // 2, count)
    return placed // TILES_X, lax.rem(placed, TILES_X)


def inside(count, row, col):
    rows = count // TILES_X
    return (row >= 0) & (row < rows) & (col >= 0) & (col < TILES_X)


def exchange_kernel(count, rims, *refs):
    n = len(rims)
    xs, tbs, lrs, cns = refs[:n], refs[n : 2 * n], refs[2 * n : 3 * n], refs[3 * n : 4 * n]
    stages, (send_sem, recv_sem) = refs[4 * n : 5 * n], refs[5 * n :]
    me = lax.axis_index("tile")
    row, col = position(count)
    barrier = pltpu.get_barrier_semaphore()
    targets = [lax.rem(me + dr * TILES_X + dc + 2 * count, count) for dr, dc in DIRS]
    for target in targets:
        pl.semaphore_signal(barrier, inc=1, device_id={"tile": target}, device_id_type=MESH)
    for x, stage in zip(xs, stages):
        width = x.shape[2]
        stage[0] = x[:, :, 0:2, :]
        stage[1] = x[:, :, width - 2 : width, :]
    pl.semaphore_wait(barrier, len(DIRS))

    def copy(a, k):
        dr, dc = DIRS[k]
        h, height = rims[a], xs[a].shape[1]
        rows = pl.ds(height - h, h) if dr == 1 else pl.ds(0, h)
        if dc == 0:
            src, dst = xs[a].at[:, rows], tbs[a].at[0 if dr == 1 else 1]
        elif dr == 0:
            src, dst = stages[a].at[1 if dc == 1 else 0], lrs[a].at[0 if dc == 1 else 1]
        else:
            src = stages[a].at[1 if dc == 1 else 0, :, rows]
            dst = cns[a].at[(0 if dr == 1 else 2) + (0 if dc == 1 else 1)]
        return pltpu.make_async_remote_copy(
            src_ref=src,
            dst_ref=dst,
            send_sem=send_sem.at[a, k],
            recv_sem=recv_sem.at[a, k],
            device_id={"tile": targets[k]},
            device_id_type=MESH,
        )

    for a in range(n):
        for k, (dr, dc) in enumerate(DIRS):

            @pl.when(inside(count, row + dr, col + dc))
            def _():
                copy(a, k).start()

    for a in range(n):
        for k, (dr, dc) in enumerate(DIRS):

            @pl.when(inside(count, row - dr, col - dc))
            def _():
                copy(a, k).wait_recv()

            @pl.when(inside(count, row + dr, col + dc))
            def _():
                copy(a, k).wait_send()


def exchange(count, arrays, rims):
    tbs, lrs, cns, stages = [], [], [], []
    for x, h in zip(arrays, rims):
        f, height, width, c = x.shape
        tbs.append(jax.ShapeDtypeStruct((2, f, h, width, c), x.dtype))
        lrs.append(jax.ShapeDtypeStruct((2, f, height, 2, c), x.dtype))
        cns.append(jax.ShapeDtypeStruct((4, f, h, 2, c), x.dtype))
        stages.append(pltpu.VMEM((2, f, height, 2, c), x.dtype))
    n = len(arrays)
    outs = pl.pallas_call(
        functools.partial(exchange_kernel, count, rims),
        out_shape=tbs + lrs + cns,
        in_specs=[pl.BlockSpec(memory_space=pltpu.VMEM)] * n,
        out_specs=[pl.BlockSpec(memory_space=pltpu.VMEM)] * (3 * n),
        scratch_shapes=stages + [pltpu.SemaphoreType.DMA((n, len(DIRS))), pltpu.SemaphoreType.DMA((n, len(DIRS)))],
        compiler_params=pltpu.CompilerParams(collective_id=0, has_side_effects=True),
        name="exchange",
    )(*arrays)
    return outs[:n], outs[n : 2 * n], outs[2 * n :]


def activate(widened, gain, channels):
    meansq = jnp.sum(widened * widened, axis=-1, keepdims=True) * (1.0 / channels)
    normed = widened * lax.rsqrt(meansq + epsilon) * gain
    return normed / (1.0 + jnp.exp(-normed))


def decode_kernel(count, *refs):
    xs = refs[0:4]
    tbs, lrs, cns = refs[4:8], refs[8:12], refs[12:16]
    w1, w2, w3, g1, g2, g3, up2, up3, out = refs[16:25]
    p1, a1, w1s, y1, p2, a2, y2, p3, dlo, dhi, sems = refs[25:]
    frames, h1, wd1, c1 = xs[0].shape
    _, h2, wd2, c2 = xs[2].shape
    _, h3, wd3, c3 = xs[3].shape
    m1 = a1.shape[1] // (h1 + 4)
    m2 = a2.shape[2] // (h2 + 4)
    copies = []
    for t in range(3):
        for b in range(3):
            for c in range(3):
                cp = pltpu.make_async_copy(w1.at[t, b, c], w1s.at[t * 3 + b, :, pl.ds(c * c1, c1)], sems.at[t, b, c])
                cp.start()
                copies.append(cp)
    row, col = position(count)
    up_ok, down_ok = row > 0, row < count // TILES_X - 1
    left_ok, right_ok = col > 0, col < TILES_X - 1

    def kept(ok, values):
        return jnp.where(ok, values, jnp.zeros_like(values))

    def place(p, at, x, tb, lr, cn, h):
        f, height, width, c = x.shape
        fs = pl.ds(at, f)
        cs = pl.ds(0, c)
        mid, lo, hi = pl.ds(h, height), pl.ds(0, h), pl.ds(h + height, h)
        inner, left, right = pl.ds(16, width), pl.ds(14, 2), pl.ds(16 + width, 2)
        p[fs, mid, inner, cs] = x[...]
        p[fs, lo, inner, cs] = kept(up_ok, tb[0])
        p[fs, hi, inner, cs] = kept(down_ok, tb[1])
        p[fs, mid, left, cs] = kept(left_ok, lr[0])
        p[fs, mid, right, cs] = kept(right_ok, lr[1])
        p[fs, lo, left, cs] = kept(up_ok & left_ok, cn[0])
        p[fs, lo, right, cs] = kept(up_ok & right_ok, cn[1])
        p[fs, hi, left, cs] = kept(down_ok & left_ok, cn[2])
        p[fs, hi, right, cs] = kept(down_ok & right_ok, cn[3])

    place(p1, 2, xs[0], tbs[0], lrs[0], cns[0], 2)
    place(p1, 0, xs[1], tbs[1], lrs[1], cns[1], 2)
    place(p2, 0, xs[2], tbs[2], lrs[2], cns[2], 2)
    place(p3, 0, xs[3], tbs[3], lrs[3], cns[3], 1)

    gain1 = g1[...]

    @pl.loop(0, frames)
    def _(f):
        for r in range(h1 + 4):
            value = p1[f + 2, r].astype(F32)
            p1[f + 2, r] = activate(value, gain1, c1).astype(BF)

    @pl.loop(0, frames + 2)
    def _(f):
        for c in range(3):
            for r in range(h1 + 4):
                a1[f, pl.ds(r * m1, m1), pl.ds(c * c1, c1)] = p1[f, r, pl.ds(14 + c, m1), :]

    for cp in copies:
        cp.wait()

    def keep_mask(rows, pitch, used):
        flat = lax.broadcasted_iota(jnp.int32, (rows * pitch, 1), 0)
        r, c = flat // pitch, lax.rem(flat, pitch)
        return r, c, used

    gain2 = g2[...]
    o1 = h1 + 2
    flat = lax.broadcasted_iota(jnp.int32, (o1 * m1, 1), 0)
    r1, q1 = flat // m1, lax.rem(flat, m1)

    def valid(r, q, rows, cols):
        top = jnp.where(up_ok, 0, 1)
        bottom = jnp.where(down_ok, rows, rows - 1)
        first = jnp.where(left_ok, 0, 1)
        last = jnp.where(right_ok, cols, cols - 1)
        return (r >= top) & (r < bottom) & (q >= first) & (q < last)

    ok1 = valid(r1, q1, o1, wd1 + 2)

    @pl.loop(0, frames)
    def _(f):
        total = jnp.zeros((o1 * m1, c2), F32)
        for t in range(3):
            for b in range(3):
                total = total + lax.dot_general(
                    a1[f + t, pl.ds(b * m1, o1 * m1), :], w1s[t * 3 + b], NT, preferred_element_type=F32
                )
        rounded = total.astype(BF).astype(F32)
        acted = jnp.where(ok1, activate(rounded, gain2, c2), 0.0).astype(BF)
        for r in range(o1):
            y1[f, :, pl.ds(r * 256, c2)] = acted[r * m1 : (r + 1) * m1]

    pitch = h2 + 4

    @pl.loop(0, 2)
    def _(f):
        for c in range(3):
            for r in range(pitch):
                a2[f, c, pl.ds(r * m2, m2), :] = p2[f, r, pl.ds(14 + c, m2), :]

    @pl.loop(0, frames)
    def _(f):
        for r in range(o1):
            wide = jnp.dot(up2[...], y1[f, :, pl.ds(r * 256, c2)], preferred_element_type=F32).astype(BF)
            for c in range(3):
                a2[f + 2, c, pl.ds(2 * r * m2, m2), :] = wide[c * m2 : (c + 1) * m2]
                a2[f + 2, c, pl.ds((2 * r + 1) * m2, m2), :] = wide[c * m2 : (c + 1) * m2]

    gain3 = g3[...]
    o2 = h2 + 2
    chunks = 3
    per = o2 // chunks
    flat2 = lax.broadcasted_iota(jnp.int32, (per * m2, 1), 0)
    r2, q2 = flat2 // m2, lax.rem(flat2, m2)
    for f0 in range(frames):
        y2[f0] = jnp.zeros(y2.shape[1:], BF)

    @pl.loop(0, frames)
    def _(f):
        for chunk in range(chunks):
            total = jnp.zeros((per * m2, c3), F32)
            for t in range(3):
                for b in range(3):
                    for c in range(3):
                        total = total + lax.dot_general(
                            a2[f + t, c, pl.ds((chunk * per + b) * m2, per * m2), :],
                            w2[t, b, c],
                            NT,
                            preferred_element_type=F32,
                        )
            rounded = total.astype(BF).astype(F32)
            ok2 = valid(r2 + chunk * per, q2, o2, wd2 + 2)
            acted = jnp.where(ok2, activate(rounded, gain3, c3), 0.0).astype(BF)
            for r in range(per):
                y2[f, chunk * per + r, :, pl.ds(0, c3)] = acted[r * m2 : (r + 1) * m2]

    taps3 = [w3[:, pl.ds(c * 128, 128)] for c in range(3)]

    @pl.loop(0, frames)
    def _(f):
        for r in range(o2):
            wide = jnp.dot(up3[...], y2[f, r], preferred_element_type=F32).astype(BF)
            total = jnp.zeros((72, wd3), F32)
            for c in range(3):
                total = total + lax.dot_general(
                    taps3[c], wide[c * wd3 : (c + 1) * wd3], NT, preferred_element_type=F32
                )
            dlo[f, r] = total

    thin3 = [w3[:, pl.ds(c * 128, c3)] for c in range(3)]

    @pl.loop(0, h3 + 2)
    def _(r):
        for f in range(2):
            total = jnp.zeros((72, wd3), F32)
            for c in range(3):
                total = total + lax.dot_general(
                    thin3[c], p3[f, r, pl.ds(15 + c, wd3), :], NT, preferred_element_type=F32
                )
            dhi[f, r] = total

    for f in range(frames):

        @pl.loop(0, h2)
        def _(i):
            for parity in range(2):
                total = None
                for t in range(3):
                    for b in range(3):
                        part = pl.ds((t * 3 + b) * 8, 8)
                        if f + t < 2:
                            term = dhi[f + t, 2 * i + parity + b, part]
                        else:
                            term = dlo[f + t - 2, i + (parity + b + 1) // 2, part]
                        total = term if total is None else total + term
                out[f, 2 * i + parity] = total


def decode(count, arrays, tbs, lrs, cns, w1, w2, w3, g1, g2, g3):
    frames, h1, wd1, c1 = arrays[0].shape
    _, h2, wd2, c2 = arrays[2].shape
    _, h3, wd3, c3 = arrays[3].shape
    m1 = -(-(wd1 + 2) // 16) * 16
    m2 = -(-(wd2 + 2) // 16) * 16
    up2 = np.zeros((3, m2, m1), np.float32)
    up3 = np.zeros((3, wd3, m2), np.float32)
    for c in range(3):
        for q in range(wd2 + 2):
            up2[c, q, (q - 1 + c - 1) // 2 + 1] = 1
        for q in range(wd3):
            up3[c, q, (q + c - 1) // 2 + 1] = 1
    up2 = jnp.asarray(up2.reshape(3 * m2, m1), BF)
    up3 = jnp.asarray(up3.reshape(3 * wd3, m2), BF)
    rgb = w3.shape[3]
    w3 = jnp.pad(w3.transpose(0, 1, 3, 2, 4), ((0, 0), (0, 0), (0, 8 - rgb), (0, 0), (0, 128 - c3))).reshape(72, 384)
    vm = pl.BlockSpec(memory_space=pltpu.VMEM)
    hbm = pl.BlockSpec(memory_space=pl.ANY)
    scratch = [
        pltpu.VMEM((frames + 2, h1 + 4, wd1 + 32, c1), BF),
        pltpu.VMEM((frames + 2, (h1 + 4) * m1, 3 * c1), BF),
        pltpu.VMEM((9, c2, 3 * c1), BF),
        pltpu.VMEM((frames, m1, (h1 + 2) * 256), BF),
        pltpu.VMEM((2, h2 + 4, wd2 + 32, c2), BF),
        pltpu.VMEM((frames + 2, 3, (h2 + 4) * m2, c2), BF),
        pltpu.VMEM((frames, h2 + 2, m2, 128), BF),
        pltpu.VMEM((2, h3 + 2, wd3 + 32, c3), BF),
        pltpu.VMEM((frames, h2 + 2, 72, wd3), F32),
        pltpu.VMEM((2, h3 + 2, 72, wd3), F32),
        pltpu.SemaphoreType.DMA((3, 3, 3)),
    ]
    out = pl.pallas_call(
        functools.partial(decode_kernel, count),
        out_shape=jax.ShapeDtypeStruct((frames, h3, 8, wd3), F32),
        in_specs=[vm] * 16 + [hbm] + [vm] * 7,
        out_specs=vm,
        scratch_shapes=scratch,
        compiler_params=pltpu.CompilerParams(vmem_limit_bytes=60 * 1024 * 1024),
        name="decode",
    )(*arrays, *tbs, *lrs, *cns, w1, w2, w3, g1[None], g2[None], g3[None], up2, up3)
    return out[:, :, :rgb].transpose(0, 2, 1, 3)


def solution(mesh):
    count = mesh.shape["tile"]

    def body(features, cache_first, cache_second, cache_third, w1, w2, w3, g1, g2, g3):
        arrays = [x[:, :, 0].transpose(0, 2, 3, 1) for x in (features, cache_first, cache_second, cache_third)]
        tbs, lrs, cns = exchange(count, arrays, (2, 2, 2, 1))
        return decode(count, arrays, tbs, lrs, cns, w1, w2, w3, g1, g2, g3)[:, :, None]

    tiled = P("groups", None, "tile", None, None)
    return jax.shard_map(
        body,
        mesh=mesh,
        in_specs=(tiled,) * 4 + (P(),) * 6,
        out_specs=tiled,
        check_vma=False,
    )
```

```python
import functools

import jax
import jax.numpy as jnp
import numpy as np
from jax import lax
from jax.experimental import pallas as pl
from jax.experimental.pallas import tpu as pltpu
from jax.sharding import PartitionSpec as P

TILES_X = 8
epsilon = 1e-06
MESH = pl.DeviceIdType.MESH
DIRS = ((1, 0), (-1, 0), (1, 1), (1, -1), (-1, 1), (-1, -1), (0, 1), (0, -1))
BF = jnp.bfloat16
F32 = jnp.float32
NT = (((1,), (1,)), ((), ()))


def position(count):
    placed = lax.rem(lax.axis_index("tile") + TILES_X // 2, count)
    return placed // TILES_X, lax.rem(placed, TILES_X)


def inside(count, row, col):
    rows = count // TILES_X
    return (row >= 0) & (row < rows) & (col >= 0) & (col < TILES_X)


def exchange_plan(count, rims, xs, tbs, lrs, cns, stages, send_sem, recv_sem):
    me = lax.axis_index("tile")
    row, col = position(count)
    barrier = pltpu.get_barrier_semaphore()
    targets = [lax.rem(me + dr * TILES_X + dc + 2 * count, count) for dr, dc in DIRS]
    for target in targets:
        pl.semaphore_signal(barrier, inc=1, device_id={"tile": target}, device_id_type=MESH)
    for x, stage in zip(xs, stages):
        width = x.shape[2]
        stage[0] = x[:, :, 0:2, :]
        stage[1] = x[:, :, width - 2 : width, :]
    pl.semaphore_wait(barrier, len(DIRS))

    def copy(a, k):
        dr, dc = DIRS[k]
        h, height = rims[a], xs[a].shape[1]
        rows = pl.ds(height - h, h) if dr == 1 else pl.ds(0, h)
        if dc == 0:
            src, dst = xs[a].at[:, rows], tbs[a].at[0 if dr == 1 else 1]
        elif dr == 0:
            src, dst = stages[a].at[1 if dc == 1 else 0], lrs[a].at[0 if dc == 1 else 1]
        else:
            src = stages[a].at[1 if dc == 1 else 0, :, rows]
            dst = cns[a].at[(0 if dr == 1 else 2) + (0 if dc == 1 else 1)]
        return pltpu.make_async_remote_copy(
            src_ref=src,
            dst_ref=dst,
            send_sem=send_sem.at[a, k],
            recv_sem=recv_sem.at[a, k],
            device_id={"tile": targets[k]},
            device_id_type=MESH,
        )

    def send(a):
        for k, (dr, dc) in enumerate(DIRS):

            @pl.when(inside(count, row + dr, col + dc))
            def _():
                copy(a, k).start()

    def receive(a):
        for k, (dr, dc) in enumerate(DIRS):

            @pl.when(inside(count, row - dr, col - dc))
            def _():
                copy(a, k).wait_recv()

    def finish(a):
        for k, (dr, dc) in enumerate(DIRS):

            @pl.when(inside(count, row + dr, col + dc))
            def _():
                copy(a, k).wait_send()

    return send, receive, finish


def activate(widened, gain, channels):
    meansq = jnp.sum(widened * widened, axis=-1, keepdims=True) * (1.0 / channels)
    normed = widened * lax.rsqrt(meansq + epsilon) * gain
    return normed / (1.0 + jnp.exp(-normed))


def decode_kernel(count, rims, *refs):
    xs = refs[0:4]
    w1, w2, w3, g1, g2, g3, up2, up3, out = refs[4:13]
    tbs, lrs, cns, stages = refs[13:17], refs[17:21], refs[21:25], refs[25:29]
    p1, a1, w1s, w2s, y1, p2, a2, y2, p3, dlo, dhi, sems, send_sem, recv_sem = refs[29:]
    frames, h1, wd1, c1 = xs[0].shape
    _, h2, wd2, c2 = xs[2].shape
    _, h3, wd3, c3 = xs[3].shape
    m1 = a1.shape[1] // (h1 + 4)
    m2 = a2.shape[2] // (h2 + 4)
    copies = []
    for t in range(3):
        for b in range(3):
            for c in range(3):
                cp = pltpu.make_async_copy(w1.at[t, b, c], w1s.at[t * 3 + b, :, pl.ds(c * c1, c1)], sems.at[t, b, c])
                cp.start()
                copies.append(cp)
    second = pltpu.make_async_copy(w2, w2s, sems.at[3, 0, 0])
    second.start()
    send, receive, finish = exchange_plan(count, rims, xs, tbs, lrs, cns, stages, send_sem, recv_sem)
    for a in (3, 0, 1, 2):
        send(a)
    row, col = position(count)
    up_ok, down_ok = row > 0, row < count // TILES_X - 1
    left_ok, right_ok = col > 0, col < TILES_X - 1

    def kept(ok, values):
        return jnp.where(ok, values, jnp.zeros_like(values))

    def place(p, at, x, tb, lr, cn, h):
        f, height, width, c = x.shape
        fs = pl.ds(at, f)
        cs = pl.ds(0, c)
        mid, lo, hi = pl.ds(h, height), pl.ds(0, h), pl.ds(h + height, h)
        inner, left, right = pl.ds(16, width), pl.ds(14, 2), pl.ds(16 + width, 2)
        p[fs, mid, inner, cs] = x[...]
        p[fs, lo, inner, cs] = kept(up_ok, tb[0])
        p[fs, hi, inner, cs] = kept(down_ok, tb[1])
        p[fs, mid, left, cs] = kept(left_ok, lr[0])
        p[fs, mid, right, cs] = kept(right_ok, lr[1])
        p[fs, lo, left, cs] = kept(up_ok & left_ok, cn[0])
        p[fs, lo, right, cs] = kept(up_ok & right_ok, cn[1])
        p[fs, hi, left, cs] = kept(down_ok & left_ok, cn[2])
        p[fs, hi, right, cs] = kept(down_ok & right_ok, cn[3])

    receive(3)
    place(p3, 0, xs[3], tbs[3], lrs[3], cns[3], 1)
    thin3 = [w3[:, pl.ds(c * 128, c3)] for c in range(3)]

    @pl.loop(0, h3 + 2)
    def _(r):
        for f in range(2):
            total = jnp.zeros((72, wd3), F32)
            for c in range(3):
                total = total + lax.dot_general(
                    thin3[c], p3[f, r, pl.ds(15 + c, wd3), :], NT, preferred_element_type=F32
                )
            dhi[f, r] = total

    receive(0)
    place(p1, 2, xs[0], tbs[0], lrs[0], cns[0], 2)
    receive(1)
    place(p1, 0, xs[1], tbs[1], lrs[1], cns[1], 2)

    gain1 = g1[...]

    @pl.loop(0, frames)
    def _(f):
        for r in range(h1 + 4):
            value = p1[f + 2, r].astype(F32)
            p1[f + 2, r] = activate(value, gain1, c1).astype(BF)

    @pl.loop(0, frames + 2)
    def _(f):
        for c in range(3):
            for r in range(h1 + 4):
                a1[f, pl.ds(r * m1, m1), pl.ds(c * c1, c1)] = p1[f, r, pl.ds(14 + c, m1), :]

    for cp in copies:
        cp.wait()

    gain2 = g2[...]
    o1 = h1 + 2
    flat = lax.broadcasted_iota(jnp.int32, (o1 * m1, 1), 0)
    r1, q1 = flat // m1, lax.rem(flat, m1)

    def valid(r, q, rows, cols):
        top = jnp.where(up_ok, 0, 1)
        bottom = jnp.where(down_ok, rows, rows - 1)
        first = jnp.where(left_ok, 0, 1)
        last = jnp.where(right_ok, cols, cols - 1)
        return (r >= top) & (r < bottom) & (q >= first) & (q < last)

    ok1 = valid(r1, q1, o1, wd1 + 2)

    @pl.loop(0, frames)
    def _(f):
        total = jnp.zeros((o1 * m1, c2), F32)
        for t in range(3):
            for b in range(3):
                total = total + lax.dot_general(
                    a1[f + t, pl.ds(b * m1, o1 * m1), :], w1s[t * 3 + b], NT, preferred_element_type=F32
                )
        rounded = total.astype(BF).astype(F32)
        acted = jnp.where(ok1, activate(rounded, gain2, c2), 0.0).astype(BF)
        for r in range(o1):
            y1[f, :, pl.ds(r * 256, c2)] = acted[r * m1 : (r + 1) * m1]

    receive(2)
    place(p2, 0, xs[2], tbs[2], lrs[2], cns[2], 2)
    pitch = h2 + 4

    @pl.loop(0, 2)
    def _(f):
        for c in range(3):
            for r in range(pitch):
                a2[f, c, pl.ds(r * m2, m2), :] = p2[f, r, pl.ds(14 + c, m2), :]

    @pl.loop(0, frames)
    def _(f):
        for r in range(o1):
            wide = jnp.dot(up2[...], y1[f, :, pl.ds(r * 256, c2)], preferred_element_type=F32).astype(BF)
            for c in range(3):
                a2[f + 2, c, pl.ds(2 * r * m2, m2), :] = wide[c * m2 : (c + 1) * m2]
                a2[f + 2, c, pl.ds((2 * r + 1) * m2, m2), :] = wide[c * m2 : (c + 1) * m2]

    second.wait()
    gain3 = g3[...]
    o2 = h2 + 2
    chunks = 3
    per = o2 // chunks
    flat2 = lax.broadcasted_iota(jnp.int32, (per * m2, 1), 0)
    r2, q2 = flat2 // m2, lax.rem(flat2, m2)
    for f0 in range(frames):
        y2[f0] = jnp.zeros(y2.shape[1:], BF)

    @pl.loop(0, frames)
    def _(f):
        for chunk in range(chunks):
            total = jnp.zeros((per * m2, c3), F32)
            for t in range(3):
                for b in range(3):
                    for c in range(3):
                        total = total + lax.dot_general(
                            a2[f + t, c, pl.ds((chunk * per + b) * m2, per * m2), :],
                            w2s[t, b, c],
                            NT,
                            preferred_element_type=F32,
                        )
            rounded = total.astype(BF).astype(F32)
            ok2 = valid(r2 + chunk * per, q2, o2, wd2 + 2)
            acted = jnp.where(ok2, activate(rounded, gain3, c3), 0.0).astype(BF)
            for r in range(per):
                y2[f, chunk * per + r, :, pl.ds(0, c3)] = acted[r * m2 : (r + 1) * m2]

    taps3 = [w3[:, pl.ds(c * 128, 128)] for c in range(3)]

    @pl.loop(0, frames)
    def _(f):
        for r in range(o2):
            wide = jnp.dot(up3[...], y2[f, r], preferred_element_type=F32).astype(BF)
            total = jnp.zeros((72, wd3), F32)
            for c in range(3):
                total = total + lax.dot_general(
                    taps3[c], wide[c * wd3 : (c + 1) * wd3], NT, preferred_element_type=F32
                )
            dlo[f, r] = total

    for f in range(frames):

        @pl.loop(0, h2)
        def _(i):
            for parity in range(2):
                total = None
                for t in range(3):
                    for b in range(3):
                        part = pl.ds((t * 3 + b) * 8, 8)
                        if f + t < 2:
                            term = dhi[f + t, 2 * i + parity + b, part]
                        else:
                            term = dlo[f + t - 2, i + (parity + b + 1) // 2, part]
                        total = term if total is None else total + term
                out[f, 2 * i + parity] = total

    for a in range(4):
        finish(a)


def decode(count, rims, arrays, w1, w2, w3, g1, g2, g3):
    frames, h1, wd1, c1 = arrays[0].shape
    _, h2, wd2, c2 = arrays[2].shape
    _, h3, wd3, c3 = arrays[3].shape
    m1 = -(-(wd1 + 2) // 16) * 16
    m2 = -(-(wd2 + 2) // 16) * 16
    up2 = np.zeros((3, m2, m1), np.float32)
    up3 = np.zeros((3, wd3, m2), np.float32)
    for c in range(3):
        for q in range(wd2 + 2):
            up2[c, q, (q - 1 + c - 1) // 2 + 1] = 1
        for q in range(wd3):
            up3[c, q, (q + c - 1) // 2 + 1] = 1
    up2 = jnp.asarray(up2.reshape(3 * m2, m1), BF)
    up3 = jnp.asarray(up3.reshape(3 * wd3, m2), BF)
    rgb = w3.shape[3]
    w3 = jnp.pad(w3.transpose(0, 1, 3, 2, 4), ((0, 0), (0, 0), (0, 8 - rgb), (0, 0), (0, 128 - c3))).reshape(72, 384)
    vm = pl.BlockSpec(memory_space=pltpu.VMEM)
    hbm = pl.BlockSpec(memory_space=pl.ANY)
    tbs, lrs, cns, stages = [], [], [], []
    for x, h in zip(arrays, rims):
        f, height, width, c = x.shape
        tbs.append(pltpu.VMEM((2, f, h, width, c), BF))
        lrs.append(pltpu.VMEM((2, f, height, 2, c), BF))
        cns.append(pltpu.VMEM((4, f, h, 2, c), BF))
        stages.append(pltpu.VMEM((2, f, height, 2, c), BF))
    scratch = tbs + lrs + cns + stages + [
        pltpu.VMEM((frames + 2, h1 + 4, wd1 + 32, c1), BF),
        pltpu.VMEM((frames + 2, (h1 + 4) * m1, 3 * c1), BF),
        pltpu.VMEM((9, c2, 3 * c1), BF),
        pltpu.VMEM(w2.shape, BF),
        pltpu.VMEM((frames, m1, (h1 + 2) * 256), BF),
        pltpu.VMEM((2, h2 + 4, wd2 + 32, c2), BF),
        pltpu.VMEM((frames + 2, 3, (h2 + 4) * m2, c2), BF),
        pltpu.VMEM((frames, h2 + 2, m2, 128), BF),
        pltpu.VMEM((2, h3 + 2, wd3 + 32, c3), BF),
        pltpu.VMEM((frames, h2 + 2, 72, wd3), F32),
        pltpu.VMEM((2, h3 + 2, 72, wd3), F32),
        pltpu.SemaphoreType.DMA((4, 3, 3)),
        pltpu.SemaphoreType.DMA((4, len(DIRS))),
        pltpu.SemaphoreType.DMA((4, len(DIRS))),
    ]
    out = pl.pallas_call(
        functools.partial(decode_kernel, count, rims),
        out_shape=jax.ShapeDtypeStruct((frames, h3, 8, wd3), F32),
        in_specs=[vm] * 4 + [hbm] * 2 + [vm] * 6,
        out_specs=vm,
        scratch_shapes=scratch,
        compiler_params=pltpu.CompilerParams(
            collective_id=0, has_side_effects=True, vmem_limit_bytes=60 * 1024 * 1024
        ),
        name="decode",
    )(*arrays, w1, w2, w3, g1[None], g2[None], g3[None], up2, up3)
    return out[:, :, :rgb].transpose(0, 2, 1, 3)


def solution(mesh):
    count = mesh.shape["tile"]

    def body(features, cache_first, cache_second, cache_third, w1, w2, w3, g1, g2, g3):
        arrays = [x[:, :, 0].transpose(0, 2, 3, 1) for x in (features, cache_first, cache_second, cache_third)]
        return decode(count, (2, 2, 2, 1), arrays, w1, w2, w3, g1, g2, g3)[:, :, None]

    tiled = P("groups", None, "tile", None, None)
    return jax.shard_map(
        body,
        mesh=mesh,
        in_specs=(tiled,) * 4 + (P(),) * 6,
        out_specs=tiled,
        check_vma=False,
    )
```

```python
import functools

import jax
import jax.numpy as jnp
import numpy as np
from jax import lax
from jax.experimental import pallas as pl
from jax.experimental.pallas import tpu as pltpu
from jax.sharding import PartitionSpec as P

TILES_X = 8
epsilon = 1e-06
MESH = pl.DeviceIdType.MESH
DIRS = ((1, 0), (-1, 0), (1, 1), (1, -1), (-1, 1), (-1, -1), (0, 1), (0, -1))
BF = jnp.bfloat16
F32 = jnp.float32
NT = (((1,), (1,)), ((), ()))


def position(count):
    placed = lax.rem(lax.axis_index("tile") + TILES_X // 2, count)
    return placed // TILES_X, lax.rem(placed, TILES_X)


def inside(count, row, col):
    rows = count // TILES_X
    return (row >= 0) & (row < rows) & (col >= 0) & (col < TILES_X)


def exchange_plan(count, rims, xs, tbs, lrs, cns, stages, send_sem, recv_sem):
    me = lax.axis_index("tile")
    row, col = position(count)
    barrier = pltpu.get_barrier_semaphore()
    targets = [lax.rem(me + dr * TILES_X + dc + 2 * count, count) for dr, dc in DIRS]
    for target in targets:
        pl.semaphore_signal(barrier, inc=1, device_id={"tile": target}, device_id_type=MESH)
    for x, stage in zip(xs, stages):
        width = x.shape[2]
        stage[0] = x[:, :, 0:2, :]
        stage[1] = x[:, :, width - 2 : width, :]
    pl.semaphore_wait(barrier, len(DIRS))

    def copy(a, k):
        dr, dc = DIRS[k]
        h, height = rims[a], xs[a].shape[1]
        rows = pl.ds(height - h, h) if dr == 1 else pl.ds(0, h)
        if dc == 0:
            src, dst = xs[a].at[:, rows], tbs[a].at[0 if dr == 1 else 1]
        elif dr == 0:
            src, dst = stages[a].at[1 if dc == 1 else 0], lrs[a].at[0 if dc == 1 else 1]
        else:
            src = stages[a].at[1 if dc == 1 else 0, :, rows]
            dst = cns[a].at[(0 if dr == 1 else 2) + (0 if dc == 1 else 1)]
        return pltpu.make_async_remote_copy(
            src_ref=src,
            dst_ref=dst,
            send_sem=send_sem.at[a, k],
            recv_sem=recv_sem.at[a, k],
            device_id={"tile": targets[k]},
            device_id_type=MESH,
        )

    def send(a):
        for k, (dr, dc) in enumerate(DIRS):

            @pl.when(inside(count, row + dr, col + dc))
            def _():
                copy(a, k).start()

    def receive(a):
        for k, (dr, dc) in enumerate(DIRS):

            @pl.when(inside(count, row - dr, col - dc))
            def _():
                copy(a, k).wait_recv()

    def finish(a):
        for k, (dr, dc) in enumerate(DIRS):

            @pl.when(inside(count, row + dr, col + dc))
            def _():
                copy(a, k).wait_send()

    return send, receive, finish


def activate(widened, gain, channels):
    meansq = jnp.sum(widened * widened, axis=-1, keepdims=True) * (1.0 / channels)
    normed = widened * lax.rsqrt(meansq + epsilon) * gain
    return normed / (1.0 + jnp.exp(-normed))


def decode_kernel(count, rims, *refs):
    xs = refs[0:4]
    w1, w2, w3, g1, g2, g3, up2, up3, out = refs[4:13]
    tbs, lrs, cns, stages = refs[13:17], refs[17:21], refs[21:25], refs[25:29]
    p1, a1, w1s, w2s, w2p, wlo, y1, p2, a2, y2, p3, dlo, dhi, sems, send_sem, recv_sem = refs[29:]
    frames, h1, wd1, c1 = xs[0].shape
    _, h2, wd2, c2 = xs[2].shape
    _, h3, wd3, c3 = xs[3].shape
    m1 = a1.shape[1] // (h1 + 4)
    m2 = a2.shape[2] // (h2 + 4)
    copies = []
    for t in range(3):
        for b in range(3):
            for c in range(3):
                cp = pltpu.make_async_copy(w1.at[t, b, c], w1s.at[t * 3 + b, :, pl.ds(c * c1, c1)], sems.at[t, b, c])
                cp.start()
                copies.append(cp)
    second = pltpu.make_async_copy(w2, w2s, sems.at[3, 0, 0])
    second.start()
    send, receive, finish = exchange_plan(count, rims, xs, tbs, lrs, cns, stages, send_sem, recv_sem)
    for a in (3, 0, 1, 2):
        send(a)
    row, col = position(count)
    up_ok, down_ok = row > 0, row < count // TILES_X - 1
    left_ok, right_ok = col > 0, col < TILES_X - 1

    def kept(ok, values):
        return jnp.where(ok, values, jnp.zeros_like(values))

    def place(p, at, x, tb, lr, cn, h):
        f, height, width, c = x.shape
        fs = pl.ds(at, f)
        cs = pl.ds(0, c)
        mid, lo, hi = pl.ds(h, height), pl.ds(0, h), pl.ds(h + height, h)
        inner, left, right = pl.ds(16, width), pl.ds(14, 2), pl.ds(16 + width, 2)
        p[fs, mid, inner, cs] = x[...]
        p[fs, lo, inner, cs] = kept(up_ok, tb[0])
        p[fs, hi, inner, cs] = kept(down_ok, tb[1])
        p[fs, mid, left, cs] = kept(left_ok, lr[0])
        p[fs, mid, right, cs] = kept(right_ok, lr[1])
        p[fs, lo, left, cs] = kept(up_ok & left_ok, cn[0])
        p[fs, lo, right, cs] = kept(up_ok & right_ok, cn[1])
        p[fs, hi, left, cs] = kept(down_ok & left_ok, cn[2])
        p[fs, hi, right, cs] = kept(down_ok & right_ok, cn[3])

    w2p[...] = jnp.zeros(w2p.shape, BF)
    second.wait()
    for t in range(3):
        for c in range(3):
            for b in range(3):
                w2p[t * 3 + c, pl.ds(b * 128, c3)] = w2s[t, b, c]
    receive(3)
    place(p3, 0, xs[3], tbs[3], lrs[3], cns[3], 1)
    thin3 = [w3[:, pl.ds(c * 128, c3)] for c in range(3)]

    @pl.loop(0, (h3 + 2) // 2)
    def _(i):
        for f in range(2):
            total = jnp.zeros((2 * wd3, 128), F32)
            for c in range(3):
                window = p3[f, pl.ds(2 * i, 2), pl.ds(15 + c, wd3), :].reshape(2 * wd3, c3)
                total = total + lax.dot_general(window, thin3[c], NT, preferred_element_type=F32)
            for r in range(2):
                dhi[f, 2 * i + r] = total[r * wd3 : (r + 1) * wd3].T[:72]

    receive(0)
    place(p1, 2, xs[0], tbs[0], lrs[0], cns[0], 2)
    receive(1)
    place(p1, 0, xs[1], tbs[1], lrs[1], cns[1], 2)

    gain1 = g1[...]

    @pl.loop(0, frames)
    def _(f):
        for r in range(h1 + 4):
            value = p1[f + 2, r].astype(F32)
            p1[f + 2, r] = activate(value, gain1, c1).astype(BF)

    @pl.loop(0, frames + 2)
    def _(f):
        for c in range(3):
            for r in range(h1 + 4):
                a1[f, pl.ds(r * m1, m1), pl.ds(c * c1, c1)] = p1[f, r, pl.ds(14 + c, m1), :]

    for cp in copies:
        cp.wait()

    gain2 = g2[...]
    o1 = h1 + 2
    flat = lax.broadcasted_iota(jnp.int32, (o1 * m1, 1), 0)
    r1, q1 = flat // m1, lax.rem(flat, m1)

    def valid(r, q, rows, cols):
        top = jnp.where(up_ok, 0, 1)
        bottom = jnp.where(down_ok, rows, rows - 1)
        first = jnp.where(left_ok, 0, 1)
        last = jnp.where(right_ok, cols, cols - 1)
        return (r >= top) & (r < bottom) & (q >= first) & (q < last)

    ok1 = valid(r1, q1, o1, wd1 + 2)

    @pl.loop(0, frames)
    def _(f):
        total = jnp.zeros((o1 * m1, c2), F32)
        for t in range(3):
            for b in range(3):
                total = total + lax.dot_general(
                    a1[f + t, pl.ds(b * m1, o1 * m1), :], w1s[t * 3 + b], NT, preferred_element_type=F32
                )
        rounded = total.astype(BF).astype(F32)
        acted = jnp.where(ok1, activate(rounded, gain2, c2), 0.0).astype(BF)
        for r in range(o1):
            y1[f, :, pl.ds(r * 256, c2)] = acted[r * m1 : (r + 1) * m1]

    receive(2)
    place(p2, 0, xs[2], tbs[2], lrs[2], cns[2], 2)
    pitch = h2 + 4

    @pl.loop(0, 2)
    def _(f):
        for c in range(3):
            for r in range(pitch):
                a2[f, c, pl.ds(r * m2, m2), :] = p2[f, r, pl.ds(14 + c, m2), :]

    @pl.loop(0, frames)
    def _(f):
        for r in range(o1):
            wide = jnp.dot(up2[...], y1[f, :, pl.ds(r * 256, c2)], preferred_element_type=F32).astype(BF)
            for c in range(3):
                a2[f + 2, c, pl.ds(2 * r * m2, m2), :] = wide[c * m2 : (c + 1) * m2]
                a2[f + 2, c, pl.ds((2 * r + 1) * m2, m2), :] = wide[c * m2 : (c + 1) * m2]

    gain3 = g3[...]
    o2 = h2 + 2
    chunks = 3
    per = o2 // chunks
    flat2 = lax.broadcasted_iota(jnp.int32, (per * m2, 1), 0)
    r2, q2 = flat2 // m2, lax.rem(flat2, m2)
    for f0 in range(frames):
        y2[f0] = jnp.zeros(y2.shape[1:], BF)

    @pl.loop(0, frames)
    def _(f):
        for chunk in range(chunks):
            pair = jnp.zeros(((per + 1) * m2, 256), F32)
            single = jnp.zeros((per * m2, 128), F32)
            for t in range(3):
                for c in range(3):
                    pair = pair + lax.dot_general(
                        a2[f + t, c, pl.ds(chunk * per * m2, (per + 1) * m2), :],
                        w2p[t * 3 + c, pl.ds(0, 256)],
                        NT,
                        preferred_element_type=F32,
                    )
            for t in range(3):
                for c in range(3):
                    single = single + lax.dot_general(
                        a2[f + t, c, pl.ds((chunk * per + 2) * m2, per * m2), :],
                        w2p[t * 3 + c, pl.ds(256, 128)],
                        NT,
                        preferred_element_type=F32,
                    )
            total = pair[: per * m2, :128] + pair[m2:, 128:] + single
            rounded = total.astype(BF).astype(F32)[:, :c3]
            ok2 = valid(r2 + chunk * per, q2, o2, wd2 + 2)
            acted = jnp.where(ok2, activate(rounded, gain3, c3), 0.0).astype(BF)
            for r in range(per):
                y2[f, chunk * per + r, :, pl.ds(0, c3)] = acted[r * m2 : (r + 1) * m2]

    taps3 = [w3[:, pl.ds(c * 128, 128)] for c in range(3)]

    @pl.loop(0, frames)
    def _(f):
        for r in range(o2):
            wide = jnp.dot(up3[...], y2[f, r], preferred_element_type=F32).astype(BF)
            for c in range(3):
                wlo[c, pl.ds(r * wd3, wd3), :] = wide[c * wd3 : (c + 1) * wd3]
        for chunk in range(chunks):
            total = jnp.zeros((per * wd3, 128), F32)
            for c in range(3):
                total = total + lax.dot_general(
                    wlo[c, pl.ds(chunk * per * wd3, per * wd3), :], taps3[c], NT, preferred_element_type=F32
                )
            for r in range(per):
                dlo[f, chunk * per + r] = total[r * wd3 : (r + 1) * wd3].T[:72]

    for f in range(frames):

        @pl.loop(0, h2)
        def _(i):
            for parity in range(2):
                total = None
                for t in range(3):
                    for b in range(3):
                        part = pl.ds((t * 3 + b) * 8, 8)
                        if f + t < 2:
                            term = dhi[f + t, 2 * i + parity + b, part]
                        else:
                            term = dlo[f + t - 2, i + (parity + b + 1) // 2, part]
                        total = term if total is None else total + term
                out[f, 2 * i + parity] = total

    for a in range(4):
        finish(a)


def decode(count, rims, arrays, w1, w2, w3, g1, g2, g3):
    frames, h1, wd1, c1 = arrays[0].shape
    _, h2, wd2, c2 = arrays[2].shape
    _, h3, wd3, c3 = arrays[3].shape
    m1 = -(-(wd1 + 2) // 16) * 16
    m2 = -(-(wd2 + 2) // 16) * 16
    up2 = np.zeros((3, m2, m1), np.float32)
    up3 = np.zeros((3, wd3, m2), np.float32)
    for c in range(3):
        for q in range(wd2 + 2):
            up2[c, q, (q - 1 + c - 1) // 2 + 1] = 1
        for q in range(wd3):
            up3[c, q, (q + c - 1) // 2 + 1] = 1
    up2 = jnp.asarray(up2.reshape(3 * m2, m1), BF)
    up3 = jnp.asarray(up3.reshape(3 * wd3, m2), BF)
    rgb = w3.shape[3]
    w3 = jnp.pad(w3.transpose(0, 1, 3, 2, 4), ((0, 0), (0, 0), (0, 8 - rgb), (0, 0), (0, 128 - c3))).reshape(72, 384)
    w3 = jnp.pad(w3, ((0, 56), (0, 0)))
    vm = pl.BlockSpec(memory_space=pltpu.VMEM)
    hbm = pl.BlockSpec(memory_space=pl.ANY)
    tbs, lrs, cns, stages = [], [], [], []
    for x, h in zip(arrays, rims):
        f, height, width, c = x.shape
        tbs.append(pltpu.VMEM((2, f, h, width, c), BF))
        lrs.append(pltpu.VMEM((2, f, height, 2, c), BF))
        cns.append(pltpu.VMEM((4, f, h, 2, c), BF))
        stages.append(pltpu.VMEM((2, f, height, 2, c), BF))
    scratch = tbs + lrs + cns + stages + [
        pltpu.VMEM((frames + 2, h1 + 4, wd1 + 32, c1), BF),
        pltpu.VMEM((frames + 2, (h1 + 4) * m1, 3 * c1), BF),
        pltpu.VMEM((9, c2, 3 * c1), BF),
        pltpu.VMEM(w2.shape, BF),
        pltpu.VMEM((9, 384, c2), BF),
        pltpu.VMEM((3, (h2 + 2) * wd3, 128), BF),
        pltpu.VMEM((frames, m1, (h1 + 2) * 256), BF),
        pltpu.VMEM((2, h2 + 4, wd2 + 32, c2), BF),
        pltpu.VMEM((frames + 2, 3, (h2 + 4) * m2, c2), BF),
        pltpu.VMEM((frames, h2 + 2, m2, 128), BF),
        pltpu.VMEM((2, h3 + 2, wd3 + 32, c3), BF),
        pltpu.VMEM((frames, h2 + 2, 72, wd3), F32),
        pltpu.VMEM((2, h3 + 2, 72, wd3), F32),
        pltpu.SemaphoreType.DMA((4, 3, 3)),
        pltpu.SemaphoreType.DMA((4, len(DIRS))),
        pltpu.SemaphoreType.DMA((4, len(DIRS))),
    ]
    out = pl.pallas_call(
        functools.partial(decode_kernel, count, rims),
        out_shape=jax.ShapeDtypeStruct((frames, h3, 8, wd3), F32),
        in_specs=[vm] * 4 + [hbm] * 2 + [vm] * 6,
        out_specs=vm,
        scratch_shapes=scratch,
        compiler_params=pltpu.CompilerParams(
            collective_id=0, has_side_effects=True, vmem_limit_bytes=60 * 1024 * 1024
        ),
        name="decode",
    )(*arrays, w1, w2, w3, g1[None], g2[None], g3[None], up2, up3)
    return out[:, :, :rgb].transpose(0, 2, 1, 3)


def solution(mesh):
    count = mesh.shape["tile"]

    def body(features, cache_first, cache_second, cache_third, w1, w2, w3, g1, g2, g3):
        arrays = [x[:, :, 0].transpose(0, 2, 3, 1) for x in (features, cache_first, cache_second, cache_third)]
        return decode(count, (2, 2, 2, 1), arrays, w1, w2, w3, g1, g2, g3)[:, :, None]

    tiled = P("groups", None, "tile", None, None)
    return jax.shard_map(
        body,
        mesh=mesh,
        in_specs=(tiled,) * 4 + (P(),) * 6,
        out_specs=tiled,
        check_vma=False,
    )
```

```python
import functools

import jax
import jax.numpy as jnp
import numpy as np
from jax import lax
from jax.experimental import pallas as pl
from jax.experimental.pallas import tpu as pltpu
from jax.sharding import PartitionSpec as P

TILES_X = 8
epsilon = 1e-06
MESH = pl.DeviceIdType.MESH
DIRS = ((1, 0), (-1, 0), (1, 1), (1, -1), (-1, 1), (-1, -1), (0, 1), (0, -1))
BF = jnp.bfloat16
F32 = jnp.float32
NT = (((1,), (1,)), ((), ()))


def position(count):
    placed = lax.rem(lax.axis_index("tile") + TILES_X // 2, count)
    return placed // TILES_X, lax.rem(placed, TILES_X)


def inside(count, row, col):
    rows = count // TILES_X
    return (row >= 0) & (row < rows) & (col >= 0) & (col < TILES_X)


def exchange_plan(count, rims, xs, tbs, lrs, cns, stages, send_sem, recv_sem):
    me = lax.axis_index("tile")
    row, col = position(count)
    barrier = pltpu.get_barrier_semaphore()
    targets = [lax.rem(me + dr * TILES_X + dc + 2 * count, count) for dr, dc in DIRS]
    for target in targets:
        pl.semaphore_signal(barrier, inc=1, device_id={"tile": target}, device_id_type=MESH)
    for x, stage in zip(xs, stages):
        width = x.shape[2]
        stage[0] = x[:, :, 0:2, :]
        stage[1] = x[:, :, width - 2 : width, :]
    pl.semaphore_wait(barrier, len(DIRS))

    def copy(a, k):
        dr, dc = DIRS[k]
        h, height = rims[a], xs[a].shape[1]
        rows = pl.ds(height - h, h) if dr == 1 else pl.ds(0, h)
        if dc == 0:
            src, dst = xs[a].at[:, rows], tbs[a].at[0 if dr == 1 else 1]
        elif dr == 0:
            src, dst = stages[a].at[1 if dc == 1 else 0], lrs[a].at[0 if dc == 1 else 1]
        else:
            src = stages[a].at[1 if dc == 1 else 0, :, rows]
            dst = cns[a].at[(0 if dr == 1 else 2) + (0 if dc == 1 else 1)]
        return pltpu.make_async_remote_copy(
            src_ref=src,
            dst_ref=dst,
            send_sem=send_sem.at[a, k],
            recv_sem=recv_sem.at[a, k],
            device_id={"tile": targets[k]},
            device_id_type=MESH,
        )

    def send(a):
        for k, (dr, dc) in enumerate(DIRS):

            @pl.when(inside(count, row + dr, col + dc))
            def _():
                copy(a, k).start()

    def receive(a, level):
        for k, (dr, dc) in enumerate(DIRS):
            if level != abs(dr):
                continue

            @pl.when(inside(count, row - dr, col - dc))
            def _():
                copy(a, k).wait_recv()

    def finish(a):
        for k, (dr, dc) in enumerate(DIRS):

            @pl.when(inside(count, row + dr, col + dc))
            def _():
                copy(a, k).wait_send()

    return send, receive, finish


def activate(widened, gain, channels):
    meansq = jnp.sum(widened * widened, axis=-1, keepdims=True) * (1.0 / channels)
    normed = widened * lax.rsqrt(meansq + epsilon) * gain
    return normed / (1.0 + jnp.exp(-normed))


def decode_kernel(count, rims, *refs):
    xs = refs[0:4]
    w1, w2, w3, g1, g2, g3, up2, up3, out = refs[4:13]
    tbs, lrs, cns, stages = refs[13:17], refs[17:21], refs[21:25], refs[25:29]
    p1, a1, w1s, w2s, w2p, wlo, y1, p2, a2, y2, p3, dlo, dhi, sems, send_sem, recv_sem = refs[29:]
    frames, h1, wd1, c1 = xs[0].shape
    _, h2, wd2, c2 = xs[2].shape
    _, h3, wd3, c3 = xs[3].shape
    m1 = a1.shape[1] // (h1 + 4)
    m2 = a2.shape[2] // (h2 + 4)
    copies = []
    for t in range(3):
        for b in range(3):
            for c in range(3):
                cp = pltpu.make_async_copy(w1.at[t, b, c], w1s.at[t * 3 + b, :, pl.ds(c * c1, c1)], sems.at[t, b, c])
                cp.start()
                copies.append(cp)
    second = pltpu.make_async_copy(w2, w2s, sems.at[3, 0, 0])
    second.start()
    send, receive, finish = exchange_plan(count, rims, xs, tbs, lrs, cns, stages, send_sem, recv_sem)
    for a in (3, 0, 1, 2):
        send(a)
    row, col = position(count)
    up_ok, down_ok = row > 0, row < count // TILES_X - 1
    left_ok, right_ok = col > 0, col < TILES_X - 1

    def kept(ok, values):
        return jnp.where(ok, values, jnp.zeros_like(values))

    def place(level, p, at, x, tb, lr, cn, h):
        f, height, width, c = x.shape
        fs = pl.ds(at, f)
        cs = pl.ds(0, c)
        mid, lo, hi = pl.ds(h, height), pl.ds(0, h), pl.ds(h + height, h)
        inner, left, right = pl.ds(16, width), pl.ds(14, 2), pl.ds(16 + width, 2)
        if level == 0:
            p[fs, mid, inner, cs] = x[...]
            p[fs, mid, left, cs] = kept(left_ok, lr[0])
            p[fs, mid, right, cs] = kept(right_ok, lr[1])
            return
        p[fs, lo, inner, cs] = kept(up_ok, tb[0])
        p[fs, hi, inner, cs] = kept(down_ok, tb[1])
        p[fs, lo, left, cs] = kept(up_ok & left_ok, cn[0])
        p[fs, lo, right, cs] = kept(up_ok & right_ok, cn[1])
        p[fs, hi, left, cs] = kept(down_ok & left_ok, cn[2])
        p[fs, hi, right, cs] = kept(down_ok & right_ok, cn[3])

    w2p[...] = jnp.zeros(w2p.shape, BF)
    second.wait()
    for t in range(3):
        for c in range(3):
            for b in range(3):
                w2p[t * 3 + c, pl.ds(b * 128, c3)] = w2s[t, b, c]
    gain1, gain2 = g1[...], g2[...]
    o1 = h1 + 2

    def prepare(rows):
        @pl.loop(0, frames)
        def _(f):
            for r in rows:
                value = p1[f + 2, r].astype(F32)
                p1[f + 2, r] = activate(value, gain1, c1).astype(BF)

        @pl.loop(0, frames + 2)
        def _(f):
            for c in range(3):
                for r in rows:
                    a1[f, pl.ds(r * m1, m1), pl.ds(c * c1, c1)] = p1[f, r, pl.ds(14 + c, m1), :]

    def valid(r, q, rows, cols):
        top = jnp.where(up_ok, 0, 1)
        bottom = jnp.where(down_ok, rows, rows - 1)
        first = jnp.where(left_ok, 0, 1)
        last = jnp.where(right_ok, cols, cols - 1)
        return (r >= top) & (r < bottom) & (q >= first) & (q < last)

    def section_one(first_frame, some, start, rows):
        size = rows * m1
        total = jnp.zeros((some * size, c2), F32)
        for t in range(3):
            for b in range(3):
                window = a1[pl.ds(first_frame + t, some), pl.ds((start + b) * m1, size), :]
                total = total + lax.dot_general(
                    window.reshape(some * size, 3 * c1), w1s[t * 3 + b], NT, preferred_element_type=F32
                )
        flat = lax.broadcasted_iota(jnp.int32, (some * size, 1), 0)
        r1, q1 = lax.rem(flat // m1, rows) + start, lax.rem(flat, m1)
        rounded = total.astype(BF).astype(F32)
        acted = jnp.where(valid(r1, q1, o1, wd1 + 2), activate(rounded, gain2, c2), 0.0).astype(BF)
        for f in range(some):
            for r in range(rows):
                part = acted[(f * rows + r) * m1 : (f * rows + r + 1) * m1]
                y1[first_frame + f, :, pl.ds((start + r) * 256, c2)] = part

    for a in range(2):
        receive(a, 0)
        place(0, p1, 2 - 2 * a, xs[a], tbs[a], lrs[a], cns[a], 2)
    prepare(range(2, h1 + 2))
    for cp in copies:
        cp.wait()

    @pl.loop(0, frames)
    def _(f):
        section_one(f, 1, 2, h1 - 2)

    receive(3, 0)
    place(0, p3, 0, xs[3], tbs[3], lrs[3], cns[3], 1)
    receive(3, 1)
    place(1, p3, 0, xs[3], tbs[3], lrs[3], cns[3], 1)
    thin3 = [w3[:, pl.ds(c * 128, c3)] for c in range(3)]

    @pl.loop(0, (h3 + 2) // 2)
    def _(i):
        for f in range(2):
            total = jnp.zeros((2 * wd3, 128), F32)
            for c in range(3):
                window = p3[f, pl.ds(2 * i, 2), pl.ds(15 + c, wd3), :].reshape(2 * wd3, c3)
                total = total + lax.dot_general(window, thin3[c], NT, preferred_element_type=F32)
            for r in range(2):
                dhi[f, 2 * i + r] = total[r * wd3 : (r + 1) * wd3].T[:72]

    for a in range(2):
        receive(a, 1)
        place(1, p1, 2 - 2 * a, xs[a], tbs[a], lrs[a], cns[a], 2)
    prepare((0, 1, h1 + 2, h1 + 3))
    section_one(0, frames, 0, 2)
    section_one(0, frames, h1, 2)

    receive(2, 0)
    place(0, p2, 0, xs[2], tbs[2], lrs[2], cns[2], 2)
    receive(2, 1)
    place(1, p2, 0, xs[2], tbs[2], lrs[2], cns[2], 2)
    pitch = h2 + 4

    @pl.loop(0, 2)
    def _(f):
        for c in range(3):
            for r in range(pitch):
                a2[f, c, pl.ds(r * m2, m2), :] = p2[f, r, pl.ds(14 + c, m2), :]

    @pl.loop(0, frames)
    def _(f):
        for r in range(o1):
            wide = jnp.dot(up2[...], y1[f, :, pl.ds(r * 256, c2)], preferred_element_type=F32).astype(BF)
            for c in range(3):
                a2[f + 2, c, pl.ds(2 * r * m2, m2), :] = wide[c * m2 : (c + 1) * m2]
                a2[f + 2, c, pl.ds((2 * r + 1) * m2, m2), :] = wide[c * m2 : (c + 1) * m2]

    gain3 = g3[...]
    o2 = h2 + 2
    chunks = 3
    per = o2 // chunks
    flat2 = lax.broadcasted_iota(jnp.int32, (per * m2, 1), 0)
    r2, q2 = flat2 // m2, lax.rem(flat2, m2)
    for f0 in range(frames):
        y2[f0] = jnp.zeros(y2.shape[1:], BF)

    @pl.loop(0, frames)
    def _(f):
        for chunk in range(chunks):
            pair = jnp.zeros(((per + 1) * m2, 256), F32)
            single = jnp.zeros((per * m2, 128), F32)
            for t in range(3):
                for c in range(3):
                    pair = pair + lax.dot_general(
                        a2[f + t, c, pl.ds(chunk * per * m2, (per + 1) * m2), :],
                        w2p[t * 3 + c, pl.ds(0, 256)],
                        NT,
                        preferred_element_type=F32,
                    )
            for t in range(3):
                for c in range(3):
                    single = single + lax.dot_general(
                        a2[f + t, c, pl.ds((chunk * per + 2) * m2, per * m2), :],
                        w2p[t * 3 + c, pl.ds(256, 128)],
                        NT,
                        preferred_element_type=F32,
                    )
            total = pair[: per * m2, :128] + pair[m2:, 128:] + single
            rounded = total.astype(BF).astype(F32)[:, :c3]
            ok2 = valid(r2 + chunk * per, q2, o2, wd2 + 2)
            acted = jnp.where(ok2, activate(rounded, gain3, c3), 0.0).astype(BF)
            for r in range(per):
                y2[f, chunk * per + r, :, pl.ds(0, c3)] = acted[r * m2 : (r + 1) * m2]

    taps3 = [w3[:, pl.ds(c * 128, 128)] for c in range(3)]

    @pl.loop(0, frames)
    def _(f):
        for r in range(o2):
            wide = jnp.dot(up3[...], y2[f, r], preferred_element_type=F32).astype(BF)
            for c in range(3):
                wlo[c, pl.ds(r * wd3, wd3), :] = wide[c * wd3 : (c + 1) * wd3]
        for chunk in range(chunks):
            total = jnp.zeros((per * wd3, 128), F32)
            for c in range(3):
                total = total + lax.dot_general(
                    wlo[c, pl.ds(chunk * per * wd3, per * wd3), :], taps3[c], NT, preferred_element_type=F32
                )
            for r in range(per):
                dlo[f, chunk * per + r] = total[r * wd3 : (r + 1) * wd3].T[:72]

    for f in range(frames):

        @pl.loop(0, h2)
        def _(i):
            for parity in range(2):
                total = None
                for t in range(3):
                    for b in range(3):
                        part = pl.ds((t * 3 + b) * 8, 8)
                        if f + t < 2:
                            term = dhi[f + t, 2 * i + parity + b, part]
                        else:
                            term = dlo[f + t - 2, i + (parity + b + 1) // 2, part]
                        total = term if total is None else total + term
                out[f, 2 * i + parity] = total

    for a in range(4):
        finish(a)


def decode(count, rims, arrays, w1, w2, w3, g1, g2, g3):
    frames, h1, wd1, c1 = arrays[0].shape
    _, h2, wd2, c2 = arrays[2].shape
    _, h3, wd3, c3 = arrays[3].shape
    m1 = -(-(wd1 + 2) // 16) * 16
    m2 = -(-(wd2 + 2) // 16) * 16
    up2 = np.zeros((3, m2, m1), np.float32)
    up3 = np.zeros((3, wd3, m2), np.float32)
    for c in range(3):
        for q in range(wd2 + 2):
            up2[c, q, (q - 1 + c - 1) // 2 + 1] = 1
        for q in range(wd3):
            up3[c, q, (q + c - 1) // 2 + 1] = 1
    up2 = jnp.asarray(up2.reshape(3 * m2, m1), BF)
    up3 = jnp.asarray(up3.reshape(3 * wd3, m2), BF)
    rgb = w3.shape[3]
    w3 = jnp.pad(w3.transpose(0, 1, 3, 2, 4), ((0, 0), (0, 0), (0, 8 - rgb), (0, 0), (0, 128 - c3))).reshape(72, 384)
    w3 = jnp.pad(w3, ((0, 56), (0, 0)))
    vm = pl.BlockSpec(memory_space=pltpu.VMEM)
    hbm = pl.BlockSpec(memory_space=pl.ANY)
    tbs, lrs, cns, stages = [], [], [], []
    for x, h in zip(arrays, rims):
        f, height, width, c = x.shape
        tbs.append(pltpu.VMEM((2, f, h, width, c), BF))
        lrs.append(pltpu.VMEM((2, f, height, 2, c), BF))
        cns.append(pltpu.VMEM((4, f, h, 2, c), BF))
        stages.append(pltpu.VMEM((2, f, height, 2, c), BF))
    scratch = tbs + lrs + cns + stages + [
        pltpu.VMEM((frames + 2, h1 + 4, wd1 + 32, c1), BF),
        pltpu.VMEM((frames + 2, (h1 + 4) * m1, 3 * c1), BF),
        pltpu.VMEM((9, c2, 3 * c1), BF),
        pltpu.VMEM(w2.shape, BF),
        pltpu.VMEM((9, 384, c2), BF),
        pltpu.VMEM((3, (h2 + 2) * wd3, 128), BF),
        pltpu.VMEM((frames, m1, (h1 + 2) * 256), BF),
        pltpu.VMEM((2, h2 + 4, wd2 + 32, c2), BF),
        pltpu.VMEM((frames + 2, 3, (h2 + 4) * m2, c2), BF),
        pltpu.VMEM((frames, h2 + 2, m2, 128), BF),
        pltpu.VMEM((2, h3 + 2, wd3 + 32, c3), BF),
        pltpu.VMEM((frames, h2 + 2, 72, wd3), F32),
        pltpu.VMEM((2, h3 + 2, 72, wd3), F32),
        pltpu.SemaphoreType.DMA((4, 3, 3)),
        pltpu.SemaphoreType.DMA((4, len(DIRS))),
        pltpu.SemaphoreType.DMA((4, len(DIRS))),
    ]
    out = pl.pallas_call(
        functools.partial(decode_kernel, count, rims),
        out_shape=jax.ShapeDtypeStruct((frames, h3, 8, wd3), F32),
        in_specs=[vm] * 4 + [hbm] * 2 + [vm] * 6,
        out_specs=vm,
        scratch_shapes=scratch,
        compiler_params=pltpu.CompilerParams(
            collective_id=0, has_side_effects=True, vmem_limit_bytes=60 * 1024 * 1024
        ),
        name="decode",
    )(*arrays, w1, w2, w3, g1[None], g2[None], g3[None], up2, up3)
    return out[:, :, :rgb].transpose(0, 2, 1, 3)


def solution(mesh):
    count = mesh.shape["tile"]

    def body(features, cache_first, cache_second, cache_third, w1, w2, w3, g1, g2, g3):
        arrays = [x[:, :, 0].transpose(0, 2, 3, 1) for x in (features, cache_first, cache_second, cache_third)]
        return decode(count, (2, 2, 2, 1), arrays, w1, w2, w3, g1, g2, g3)[:, :, None]

    tiled = P("groups", None, "tile", None, None)
    return jax.shard_map(
        body,
        mesh=mesh,
        in_specs=(tiled,) * 4 + (P(),) * 6,
        out_specs=tiled,
        check_vma=False,
    )
```
